512 devices in a mesh: tm: 16 (over y, x_lo, core), chan: 32 (over z, x_hi).
Axes of the slice: x: 4 (x_hi: 2, x_lo: 2; x = x_hi * 2 + x_lo), y: 4, z: 16, core: 2. Of those that a mesh axis runs over, the one named last changes fastest.
Arguments:
- raw: bfloat16 [16384, 4096], P('tm', 'chan'), may hold values from -6 to 6
- taps: bfloat16 [512], replicated, may hold values from -0.25 to 0.25
Outputs:
- correlations: float32 [4096, 64, 1024], P('chan', 'tm')
The draws below stay inside these ranges and needn't reach their ends.
All inputs are finite; a program needn't handle non-finite values.
Results may differ from the reference program's by a relative error of at most 0.0044.
Values may be sent and summed in bfloat16 or wider, within the bound.
No kernel may reach another device: no remote copies, remote signals or barrier semaphores. Data moves between devices by JAX's collectives and lax.ppermute only.
A program may use at most 128 MiB of HBM per device.

```python
import math
import jax
import jax.numpy as jnp
from jax import lax

C = 4096
TAPS = 512
HW = 64
FR = 1024
NT = 16384
NFRAME = 16
NSRC = 64
LAGS = 1024


def shard_levels(own_key, dims, pieces, least, largest):
    factor_of = 1.0
    for position, blocks in pieces:
        steps = jax.random.uniform(jax.random.fold_in(jax.random.fold_in(own_key, 6), position), (blocks,), jnp.float32, least / len(pieces), largest / len(pieces))
        factor_of = factor_of * jnp.repeat(jnp.exp(steps), dims[position] // blocks).reshape((-1,) + (1,) * (len(dims) - 1 - position))
    return factor_of


def centred(rng, shape, deviation, reach, split=(), kind=jnp.bfloat16):
    entries = jax.random.normal(rng, shape, jnp.float32) * deviation
    if len(split) > 0:
        entries = shard_levels(rng, shape, split, -0.22, 0.18) * entries
    return jnp.clip(entries, min=-reach, max=reach).astype(kind)


def setup_inputs(seed: int = 0) -> dict:
    splits = jax.random.split(jax.random.key(seed), 3)
    return {
        "raw": centred(splits[0], (NT, C), 1.0, 6.0, ((0, 16), (1, 32))),
        "taps": centred(splits[1], (TAPS,), TAPS ** -0.5, 0.25),
    }


epsilon = 1e-05

def reference(raw, taps):
    block = 128
    kernel = taps.astype(jnp.float32)[::-1]
    length = NT + TAPS
    kernel_spec = jnp.fft.rfft(kernel, n=length)

    def prepare(columns):
        data = columns.astype(jnp.float32)
        product = jnp.fft.rfft(data, n=length, axis=0) * kernel_spec[:, None]
        filtered = jnp.fft.irfft(product, n=length, axis=0)[:NT]
        padded = jnp.pad(jnp.abs(filtered), ((HW, HW), (0, 0)))
        total = lax.reduce_window(padded, jnp.zeros((), padded.dtype), lax.add, (2 * HW + 1, 1), (1, 1), 'VALID')
        level = total / (2 * HW + 1)
        whitened = (filtered / (level + epsilon)).astype(jnp.bfloat16)
        frames = whitened.astype(jnp.float32).reshape(NFRAME, FR, block)
        spectrum = jnp.fft.rfft(frames, n=2 * FR, axis=1)[:, :FR]
        return (jnp.real(spectrum).astype(jnp.bfloat16), jnp.imag(spectrum).astype(jnp.bfloat16))
    columns = raw.reshape(NT, C // block, block).transpose(1, 0, 2)
    spec_re, spec_im = lax.map(prepare, columns)
    stride = C // NSRC
    whole_re = spec_re.transpose(1, 2, 0, 3).reshape(NFRAME, FR, C)[:, :, ::stride].astype(jnp.float32)
    whole_im = spec_im.transpose(1, 2, 0, 3).reshape(NFRAME, FR, C)[:, :, ::stride].astype(jnp.float32)
    scale = 1.0 / math.sqrt(NFRAME * FR)
    highest = lax.Precision.HIGHEST

    def correlate(pair):
        part_re = pair[0].astype(jnp.float32)
        part_im = pair[1].astype(jnp.float32)
        real_part = jnp.einsum('bfs,bfc->csf', whole_re, part_re, precision=highest) + jnp.einsum('bfs,bfc->csf', whole_im, part_im, precision=highest)
        imag_part = jnp.einsum('bfs,bfc->csf', whole_re, part_im, precision=highest) - jnp.einsum('bfs,bfc->csf', whole_im, part_re, precision=highest)
        spectrum = lax.complex(real_part, imag_part)
        spectrum = jnp.concatenate([spectrum, jnp.zeros((block, NSRC, 1), spectrum.dtype)], axis=2)
        wave = jnp.fft.irfft(spectrum, n=2 * FR, axis=2)
        lagged = jnp.concatenate([wave[:, :, 2 * FR - LAGS // 2:], wave[:, :, :LAGS // 2]], axis=2)
        return lagged * scale
    result = lax.map(correlate, (spec_re, spec_im))
    return result.reshape(C, NSRC, LAGS)
```

```python
import functools
import math

import jax
import jax.numpy as jnp
from jax import lax
from jax.experimental import pallas as pl
from jax.experimental.pallas import tpu as pltpu
from jax.sharding import PartitionSpec as P

TAPS = 512
HW = 64
FR = 1024
LAGS = 1024
SRC_DEV = 2
BEFORE = 640
AFTER = 128
TILE = 256
EPS = 1e-05
BF16 = jnp.bfloat16
F32 = jnp.float32


def dot(a, b):
    return jnp.dot(a, b, preferred_element_type=F32)


def strip(row, first, store):
    width = row.shape[1]
    base = pltpu.roll(jnp.broadcast_to(row, (8, width)), first, 1, stride=1, stride_axis=0)
    for h in range(8):
        low = pltpu.roll(base, 16 * h, 1) if h else base
        high = pltpu.roll(base, 16 * h + 8, 1)
        store(h, jnp.concatenate([low, high], 0).astype(BF16))


def whiten_kernel(
    last_ref, before_ref, raw_ref, after_ref, taps_ref, white_ref, src_ref, toep_ref, rawt_ref, filt_ref
):
    channels = raw_ref.shape[1]
    toep_rows = TAPS + TILE

    def store(h, rows):
        for a in range(toep_rows // 128):
            at = BEFORE - 128 * a
            toep_ref[128 * a + 16 * h : 128 * a + 16 * h + 16, :] = rows[:, at : at + TILE]

    strip(taps_ref[...], 0, store)
    rawt_ref[:, :BEFORE] = before_ref[...].T
    rawt_ref[:, BEFORE : BEFORE + FR] = raw_ref[...].T
    rawt_ref[:, BEFORE + FR :] = after_ref[...].T
    toep = toep_ref[...]
    span = FR + 2 * AFTER
    for y in range(0, span, TILE):
        filt_ref[:, y : y + TILE] = dot(rawt_ref[:, y : y + toep_rows], toep)
    past = lax.broadcasted_iota(jnp.int32, (channels, AFTER), 0) * 0 + last_ref[0]
    filt_ref[:, span - AFTER :] = jnp.where(past == 1, 0.0, filt_ref[:, span - AFTER :])
    size = jnp.abs(filt_ref[...])
    hi = size.astype(BF16)
    lo = (size - hi.astype(F32)).astype(BF16)
    gap = lax.broadcasted_iota(jnp.int32, (2 * TILE, TILE), 0) - lax.broadcasted_iota(
        jnp.int32, (2 * TILE, TILE), 1
    )
    band = jnp.where((gap >= AFTER - HW) & (gap <= AFTER + HW), 1.0, 0.0).astype(BF16)
    stride = channels // SRC_DEV
    row = lax.broadcasted_iota(jnp.int32, (16, channels), 0)
    col = lax.broadcasted_iota(jnp.int32, (16, channels), 1)
    pick = jnp.where((col == row * stride) & (row < SRC_DEV), 1.0, 0.0).astype(BF16)
    r = lax.broadcasted_iota(jnp.int32, (128, 128), 0)
    c = lax.broadcasted_iota(jnp.int32, (128, 128), 1)
    flip = jnp.where(r + c == 127, 1.0, 0.0).astype(BF16)
    for t in range(0, FR, TILE):
        total = dot(hi[:, t : t + 2 * TILE], band) + dot(lo[:, t : t + 2 * TILE], band)
        level = total / (2 * HW + 1)
        center = filt_ref[:, AFTER + t : AFTER + t + TILE]
        white = (center / (level + EPS)).astype(BF16)
        for u in range(0, TILE, 128):
            q = (t + u) // 128
            part = white[:, u : u + 128]
            white_ref[channels * q : channels * (q + 1), :] = part
            back = dot(dot(pick, part).astype(BF16), flip).astype(BF16)
            for k in range(SRC_DEV):
                at = k * (FR // 128) + FR // 128 - 1 - q
                src_ref[at : at + 1, :] = back[k : k + 1]


def correlate_kernel(
    base_ref, white_ref, src_ref, out_ref, lhs_ref, nyq_ref, toep0_ref, toep1_ref, acc_ref, *, scale
):
    frames = white_ref.shape[0]
    count, channels, _ = out_ref.shape
    blocks = FR // TILE
    toeps = (toep0_ref, toep1_ref)
    pad = jnp.zeros((1, TILE), F32)

    def build(s):
        to_ref = toeps[s % 2]
        own = src_ref[s]
        for b in range(frames):

            def store(h, rows, b=b):
                at = TILE * b + 16 * h
                to_ref[at : at + 16, :] = rows[:, TILE:]
                to_ref[at + 128 : at + 144, :] = rows[:, TILE - 128 : -128]

            strip(jnp.concatenate([pad, own[b : b + 1], pad], 1), 1, store)

    sign = 1.0 - 2.0 * (lax.broadcasted_iota(jnp.int32, (128, 128), 0) % 2).astype(F32)
    alternate = sign.astype(BF16)
    build(0)
    for b in range(frames):
        nyq = jnp.zeros((channels, 128), F32)
        for q in range(FR // 128):
            part = white_ref[b, channels * q : channels * (q + 1), :]
            to = channels * (q // 2)
            at = TILE * b + 128 * (q % 2)
            lhs_ref[to : to + channels, at : at + 128] = part
            nyq += dot(part, alternate)
        nyq_ref[b] = nyq

    for s in range(count):
        if s + 1 < count:
            build(s + 1)
        toep_ref = toeps[s % 2]
        for d in (0, 1, -1, 2, -2):
            at = TILE * (2 - d)
            first = channels * max(d, 0)
            rows = channels * (blocks - abs(d))
            res = dot(lhs_ref[first : first + rows, :], toep_ref[:, at : at + TILE])
            to = channels * max(-d, 0)
            if d == 0:
                acc_ref[...] = res
            else:
                acc_ref[to : to + rows, :] += res

        own = src_ref[s]
        lane = lax.broadcasted_iota(jnp.int32, (frames, FR), 1)
        own_nyq = jnp.sum(jnp.where(lane % 2 == 1, own, -own), axis=1, keepdims=True)
        nyq = own_nyq[0:1] * nyq_ref[0]
        for b in range(1, frames):
            nyq += own_nyq[b : b + 1] * nyq_ref[b]
        lane = lax.broadcasted_iota(jnp.int32, (channels, 128), 1)
        nyq = jnp.where(lane % 2 == 1, -nyq, nyq) * (scale / (2 * FR))
        nyq = jnp.concatenate([nyq] * (TILE // 128), 1)
        for j in range(blocks):
            part = acc_ref[channels * j : channels * (j + 1), :] * scale - nyq
            out_ref[s, :, TILE * j : TILE * (j + 1)] = part.astype(out_ref.dtype)


def correlate(base, bundle, src, channels, count, scale, dtype):
    frames = bundle.shape[0]
    rows = channels * (FR // 128)
    return pl.pallas_call(
        functools.partial(correlate_kernel, scale=scale),
        out_shape=jax.ShapeDtypeStruct((count, channels, LAGS), dtype),
        grid_spec=pltpu.PrefetchScalarGridSpec(
            num_scalar_prefetch=1,
            grid=(1,),
            in_specs=[
                pl.BlockSpec((frames, rows, 128), lambda i, base: (0, 0, 0)),
                pl.BlockSpec((count, frames, FR), lambda i, base: (base[0], 0, 0)),
            ],
            out_specs=pl.BlockSpec((count, channels, LAGS), lambda i, base: (0, 0, 0)),
            scratch_shapes=[
                pltpu.VMEM((FR // TILE * channels, TILE * frames), BF16),
                pltpu.VMEM((frames, channels, 128), F32),
                pltpu.VMEM((TILE * frames, 5 * TILE), BF16),
                pltpu.VMEM((TILE * frames, 5 * TILE), BF16),
                pltpu.VMEM((FR // TILE * channels, TILE), F32),
            ],
        ),
        compiler_params=pltpu.CompilerParams(vmem_limit_bytes=50 << 20),
    )(base, bundle, src)


def finish_kernel(ours_ref, theirs_ref, out_ref):
    count, channels, _ = ours_ref.shape
    for s in range(count):
        for q in range(LAGS // 128):
            lanes = slice(128 * q, 128 * (q + 1))
            both = ours_ref[s, :, lanes] + theirs_ref[s, :, lanes].astype(F32)
            out_ref[pl.ds(count * q + s, channels, stride=count * LAGS // 128), :] = both


def finish(ours, theirs):
    count, channels, _ = ours.shape
    out = pl.pallas_call(
        finish_kernel,
        out_shape=jax.ShapeDtypeStruct((channels * LAGS // 128 * count, 128), F32),
        compiler_params=pltpu.CompilerParams(vmem_limit_bytes=50 << 20),
    )(ours, theirs)
    out = out.reshape(channels, LAGS // 128, count, 128).transpose(0, 2, 1, 3)
    return out.reshape(channels, count, LAGS)


def on_device(raw, taps):
    samples, channels = raw.shape
    time_parts = lax.axis_size("tm")
    chan_parts = lax.axis_size("chan")
    chips = time_parts // 2
    place = lax.axis_index("tm")
    core = place % 2
    sources = SRC_DEV * chan_parts // chips
    scale = 1.0 / math.sqrt(samples * time_parts)
    up = [(i, i + 1) for i in range(time_parts - 1)]
    down = [(i + 1, i) for i in range(time_parts - 1)]
    before = lax.ppermute(raw[samples - BEFORE :], "tm", up)
    after = lax.ppermute(raw[:AFTER], "tm", down)
    last = (place == time_parts - 1).astype(jnp.int32).reshape(1)
    taps_row = jnp.concatenate(
        [jnp.zeros((128,), F32), taps[::-1].astype(F32), jnp.zeros((384,), F32)]
    )[None]
    frame_rows = FR // 128
    whole = pl.BlockSpec(memory_space=pltpu.VMEM)
    white, src = pl.pallas_call(
        whiten_kernel,
        out_shape=(
            jax.ShapeDtypeStruct((frame_rows * channels, 128), BF16),
            jax.ShapeDtypeStruct((SRC_DEV * frame_rows, 128), BF16),
        ),
        in_specs=[pl.BlockSpec(memory_space=pltpu.SMEM), whole, whole, whole, whole],
        scratch_shapes=[
            pltpu.VMEM((TAPS + TILE, TILE), BF16),
            pltpu.VMEM((channels, BEFORE + FR + AFTER), BF16),
            pltpu.VMEM((channels, FR + 2 * AFTER), F32),
        ],
        compiler_params=pltpu.CompilerParams(vmem_limit_bytes=50 << 20),
    )(last, before, raw, after, taps_row)
    every = lax.all_to_all(
        jnp.broadcast_to(src[None], (chan_parts,) + src.shape), "chan", 0, 0, tiled=True
    )
    every = every.reshape(chips, sources * frame_rows, 128)
    bundle = jnp.concatenate([jnp.broadcast_to(white[None], (chips,) + white.shape), every], 1)
    groups = [[c + 2 * i for i in range(chips)] for c in range(2)]
    bundle = lax.all_to_all(bundle, "tm", 0, 0, tiled=True, axis_index_groups=groups)
    srcs = bundle[:, frame_rows * channels :].astype(F32)
    srcs = srcs.reshape(chips, sources, FR).transpose(1, 0, 2)
    half = sources // 2
    theirs = correlate((1 - core).reshape(1), bundle, srcs, channels, half, scale, BF16)
    theirs = lax.ppermute(theirs, "tm", [(i, i ^ 1) for i in range(time_parts)])
    ours = correlate(core.reshape(1), bundle, srcs, channels, half, scale, F32)
    return finish(ours, theirs)


def solution(mesh):
    placed = (P("tm", "chan"), P())
    return jax.shard_map(
        on_device, mesh=mesh, in_specs=placed, out_specs=P("chan", "tm", None), check_vma=False
    )
```

```python
import functools
import math

import jax
import jax.numpy as jnp
from jax import lax
from jax.experimental import pallas as pl
from jax.experimental.pallas import tpu as pltpu
from jax.sharding import PartitionSpec as P

TAPS = 512
HW = 64
FR = 1024
LAGS = 1024
SRC_DEV = 2
BEFORE = 640
AFTER = 128
TILE = 256
EPS = 1e-05
BF16 = jnp.bfloat16
F32 = jnp.float32


def dot(a, b):
    return jnp.dot(a, b, preferred_element_type=F32)


def strip(row, first, store):
    width = row.shape[1]
    base = pltpu.roll(jnp.broadcast_to(row, (8, width)), first, 1, stride=1, stride_axis=0)
    for h in range(8):
        low = pltpu.roll(base, 16 * h, 1) if h else base
        high = pltpu.roll(base, 16 * h + 8, 1)
        store(h, jnp.concatenate([low, high], 0).astype(BF16))


def whiten_kernel(
    last_ref, before_ref, raw_ref, after_ref, taps_ref, white_ref, src_ref, toep_ref, rawt_ref, filt_ref
):
    channels = raw_ref.shape[1]
    toep_rows = TAPS + TILE
    r = lax.broadcasted_iota(jnp.int32, (128, 128), 0)
    c = lax.broadcasted_iota(jnp.int32, (128, 128), 1)
    flip = jnp.where(r + c == 127, 1.0, 0.0).astype(BF16)
    taps = jnp.broadcast_to(taps_ref[...].astype(F32), (16, TAPS)).astype(BF16)
    parts = [jnp.zeros((1, 128), F32)]
    parts += [dot(taps[:, t - 128 : t], flip)[:1] for t in range(TAPS, 0, -128)]
    parts += [jnp.zeros((1, 384), F32)]

    def store(h, rows):
        for a in range(toep_rows // 128):
            at = BEFORE - 128 * a
            toep_ref[128 * a + 16 * h : 128 * a + 16 * h + 16, :] = rows[:, at : at + TILE]

    strip(jnp.concatenate(parts, 1), 0, store)
    rawt_ref[:, :BEFORE] = before_ref[FR - BEFORE :, :].T
    rawt_ref[:, BEFORE : BEFORE + FR] = raw_ref[...].T
    rawt_ref[:, BEFORE + FR :] = after_ref[...].T
    toep = toep_ref[...]
    span = FR + 2 * AFTER
    for y in range(0, span, TILE):
        filt_ref[:, y : y + TILE] = dot(rawt_ref[:, y : y + toep_rows], toep)
    past = lax.broadcasted_iota(jnp.int32, (channels, AFTER), 0) * 0 + last_ref[0]
    filt_ref[:, span - AFTER :] = jnp.where(past == 1, 0.0, filt_ref[:, span - AFTER :])
    size = jnp.abs(filt_ref[...])
    hi = size.astype(BF16)
    lo = (size - hi.astype(F32)).astype(BF16)
    gap = lax.broadcasted_iota(jnp.int32, (2 * TILE, TILE), 0) - lax.broadcasted_iota(
        jnp.int32, (2 * TILE, TILE), 1
    )
    band = jnp.where((gap >= AFTER - HW) & (gap <= AFTER + HW), 1.0, 0.0).astype(BF16)
    stride = channels // SRC_DEV
    row = lax.broadcasted_iota(jnp.int32, (16, channels), 0)
    col = lax.broadcasted_iota(jnp.int32, (16, channels), 1)
    pick = jnp.where((col == row * stride) & (row < SRC_DEV), 1.0, 0.0).astype(BF16)
    for t in range(0, FR, TILE):
        total = dot(hi[:, t : t + 2 * TILE], band) + dot(lo[:, t : t + 2 * TILE], band)
        level = total / (2 * HW + 1)
        center = filt_ref[:, AFTER + t : AFTER + t + TILE]
        white = (center / (level + EPS)).astype(BF16)
        for u in range(0, TILE, 128):
            q = (t + u) // 128
            part = white[:, u : u + 128]
            white_ref[channels * q : channels * (q + 1), :] = part
            back = dot(dot(pick, part).astype(BF16), flip).astype(BF16)
            for k in range(SRC_DEV):
                at = k * (FR // 128) + FR // 128 - 1 - q
                src_ref[at : at + 1, :] = back[k : k + 1]


def correlate_kernel(
    half_ref, white_ref, src_ref, out_ref, lhs_ref, nyq_ref, toep0_ref, toep1_ref, acc_ref, *rest, scale
):
    frames = white_ref.shape[0]
    channels = nyq_ref.shape[1]
    count = src_ref.shape[0] // 2
    to_rows = rest[0] if rest else out_ref
    base = half_ref[0] * count
    blocks = FR // TILE
    toeps = (toep0_ref, toep1_ref)
    pad = jnp.zeros((1, TILE), F32)

    def build(s, b):
        to_ref = toeps[s % 2]
        row = src_ref[base + s, b : b + 1, :]

        def store(h, rows):
            at = TILE * b + 16 * h
            to_ref[at : at + 16, :] = rows[:, TILE:]
            to_ref[at + 128 : at + 144, :] = rows[:, TILE - 128 : -128]

        strip(jnp.concatenate([pad, row, pad], 1), 1, store)

    odd = lax.broadcasted_iota(jnp.int32, (channels, 128), 1) % 2 == 1
    for b in range(frames):
        build(0, b)
        total = jnp.zeros((channels, 128), F32)
        for q in range(FR // 128):
            part = white_ref[b, channels * q : channels * (q + 1), :]
            to = channels * (q // 2)
            at = TILE * b + 128 * (q % 2)
            lhs_ref[to : to + channels, at : at + 128] = part
            total += part.astype(F32)
        nyq_ref[b] = jnp.sum(jnp.where(odd, -total, total), axis=1, keepdims=True)

    for s in range(count):
        toep_ref = toeps[s % 2]
        todo = list(range(frames)) if s + 1 < count else []
        for d in (0, 1, -1, 2, -2):
            at = TILE * (2 - d)
            first = channels * max(d, 0)
            rows = channels * (blocks - abs(d))
            res = dot(lhs_ref[first : first + rows, :], toep_ref[:, at : at + TILE])
            to = channels * max(-d, 0)
            if d == 0:
                acc_ref[...] = res
            else:
                acc_ref[to : to + rows, :] += res
            for b in todo[:2]:
                build(s + 1, b)
            todo = todo[2:]

        own = src_ref[base + s]
        lane = lax.broadcasted_iota(jnp.int32, (frames, FR), 1)
        own_nyq = jnp.sum(jnp.where(lane % 2 == 1, own, -own), axis=1, keepdims=True)
        nyq = own_nyq[0:1] * nyq_ref[0]
        for b in range(1, frames):
            nyq += own_nyq[b : b + 1] * nyq_ref[b]
        nyq = jnp.broadcast_to(nyq, (channels, 128))
        nyq = jnp.where(odd, -nyq, nyq) * (scale / (2 * FR))
        nyq = jnp.concatenate([nyq] * (TILE // 128), 1)
        for j in range(blocks):
            part = acc_ref[channels * j : channels * (j + 1), :] * scale - nyq
            for u in range(TILE // 128):
                at = count * (TILE // 128 * j + u) + s
                rows = pl.ds(at, channels, stride=count * (LAGS // 128))
                to_rows[rows, :] = part[:, 128 * u : 128 * (u + 1)]
    if rest:
        out_ref[...] = to_rows[...].astype(out_ref.dtype)


def correlate(half, bundle, src, channels, scale, dtype):
    frames = bundle.shape[0]
    count = src.shape[0] // 2
    shape = (channels * LAGS // 128 * count, 128)
    whole = pl.BlockSpec(memory_space=pltpu.VMEM)
    scratch = [
        pltpu.VMEM((FR // TILE * channels, TILE * frames), BF16),
        pltpu.VMEM((frames, channels, 1), F32),
        pltpu.VMEM((TILE * frames, 5 * TILE), BF16),
        pltpu.VMEM((TILE * frames, 5 * TILE), BF16),
        pltpu.VMEM((FR // TILE * channels, TILE), F32),
    ]
    if dtype != F32:
        scratch.append(pltpu.VMEM(shape, F32))
    return pl.pallas_call(
        functools.partial(correlate_kernel, scale=scale),
        out_shape=jax.ShapeDtypeStruct(shape, dtype),
        in_specs=[pl.BlockSpec(memory_space=pltpu.SMEM), whole, whole],
        out_specs=whole,
        scratch_shapes=scratch,
        compiler_params=pltpu.CompilerParams(vmem_limit_bytes=36 << 20),
    )(half, bundle, src)


def on_device(raw, taps):
    samples, channels = raw.shape
    time_parts = lax.axis_size("tm")
    chan_parts = lax.axis_size("chan")
    chips = time_parts // 2
    place = lax.axis_index("tm")
    core = place % 2
    sources = SRC_DEV * chan_parts // chips
    scale = 1.0 / math.sqrt(samples * time_parts)
    up = [(i, i + 1) for i in range(time_parts - 1)]
    down = [(i + 1, i) for i in range(time_parts - 1)]
    before = lax.ppermute(raw, "tm", up)
    after = lax.ppermute(raw[:AFTER], "tm", down)
    last = (place == time_parts - 1).astype(jnp.int32).reshape(1)
    frame_rows = FR // 128
    whole = pl.BlockSpec(memory_space=pltpu.VMEM)
    white, src = pl.pallas_call(
        whiten_kernel,
        out_shape=(
            jax.ShapeDtypeStruct((frame_rows * channels, 128), BF16),
            jax.ShapeDtypeStruct((SRC_DEV * frame_rows, 128), BF16),
        ),
        grid=(1,),
        in_specs=[
            pl.BlockSpec(memory_space=pltpu.SMEM),
            whole,
            pl.BlockSpec((samples, channels), lambda i: (0, 0)),
            whole,
            pl.BlockSpec((1, TAPS), lambda i: (0, 0)),
        ],
        out_specs=(whole, whole),
        scratch_shapes=[
            pltpu.VMEM((TAPS + TILE, TILE), BF16),
            pltpu.VMEM((channels, BEFORE + FR + AFTER), BF16),
            pltpu.VMEM((channels, FR + 2 * AFTER), F32),
        ],
        compiler_params=pltpu.CompilerParams(vmem_limit_bytes=50 << 20),
    )(last, before, raw, after, taps[None])
    every = lax.all_to_all(
        jnp.broadcast_to(src[None], (chan_parts,) + src.shape), "chan", 0, 0, tiled=True
    )
    every = every.reshape(chips, sources * frame_rows, 128)
    bundle = jnp.concatenate([jnp.broadcast_to(white[None], (chips,) + white.shape), every], 1)
    groups = [[c + 2 * i for i in range(chips)] for c in range(2)]
    bundle = lax.all_to_all(bundle, "tm", 0, 0, tiled=True, axis_index_groups=groups)
    srcs = bundle[:, frame_rows * channels :].astype(F32)
    srcs = srcs.reshape(chips, sources, FR).transpose(1, 0, 2)
    theirs = correlate((1 - core).reshape(1), bundle, srcs, channels, scale, BF16)
    theirs = lax.ppermute(theirs, "tm", [(i, i ^ 1) for i in range(time_parts)])
    ours = correlate(core.reshape(1), bundle, srcs, channels, scale, F32)
    out = ours + theirs.astype(F32)
    out = out.reshape(channels, LAGS // 128, sources // 2, 128).transpose(0, 2, 1, 3)
    return out.reshape(channels, sources // 2, LAGS)


def solution(mesh):
    placed = (P("tm", "chan"), P())
    return jax.shard_map(
        on_device, mesh=mesh, in_specs=placed, out_specs=P("chan", "tm", None), check_vma=False
    )
```

```python
import functools
import math

import jax
import jax.numpy as jnp
from jax import lax
from jax.experimental import pallas as pl
from jax.experimental.pallas import tpu as pltpu
from jax.sharding import PartitionSpec as P

TAPS = 512
HW = 64
FR = 1024
LAGS = 1024
SRC_DEV = 2
BEFORE = 640
AFTER = 128
TILE = 256
EPS = 1e-05
BF16 = jnp.bfloat16
F32 = jnp.float32


def dot(a, b):
    return jnp.dot(a, b, preferred_element_type=F32)


def strip(row, first, store):
    width = row.shape[1]
    base = pltpu.roll(jnp.broadcast_to(row, (8, width)), first, 1, stride=1, stride_axis=0)
    for h in range(8):
        low = pltpu.roll(base, 16 * h, 1) if h else base
        high = pltpu.roll(base, 16 * h + 8, 1)
        store(h, jnp.concatenate([low, high], 0).astype(BF16))


def whiten_kernel(
    last_ref, before_ref, raw_ref, after_ref, taps_ref, white_ref, src_ref, toep_ref, rawt_ref, filt_ref
):
    channels = raw_ref.shape[1]
    toep_rows = TAPS + TILE
    r = lax.broadcasted_iota(jnp.int32, (128, 128), 0)
    c = lax.broadcasted_iota(jnp.int32, (128, 128), 1)
    flip = jnp.where(r + c == 127, 1.0, 0.0).astype(BF16)
    taps = jnp.broadcast_to(taps_ref[...].astype(F32), (16, TAPS)).astype(BF16)
    parts = [jnp.zeros((1, 128), F32)]
    parts += [dot(taps[:, t - 128 : t], flip)[:1] for t in range(TAPS, 0, -128)]
    parts += [jnp.zeros((1, 384), F32)]

    def store(h, rows):
        for a in range(toep_rows // 128):
            at = BEFORE - 128 * a
            toep_ref[128 * a + 16 * h : 128 * a + 16 * h + 16, :] = rows[:, at : at + TILE]

    strip(jnp.concatenate(parts, 1), 0, store)
    rawt_ref[:, :BEFORE] = before_ref[FR - BEFORE :, :].T
    rawt_ref[:, BEFORE : BEFORE + FR] = raw_ref[...].T
    rawt_ref[:, BEFORE + FR :] = after_ref[...].T
    toep = toep_ref[...]
    span = FR + 2 * AFTER
    for y in range(0, span, TILE):
        filt_ref[:, y : y + TILE] = dot(rawt_ref[:, y : y + toep_rows], toep)
    past = lax.broadcasted_iota(jnp.int32, (channels, AFTER), 0) * 0 + last_ref[0]
    filt_ref[:, span - AFTER :] = jnp.where(past == 1, 0.0, filt_ref[:, span - AFTER :])
    size = jnp.abs(filt_ref[...])
    hi = size.astype(BF16)
    lo = (size - hi.astype(F32)).astype(BF16)
    gap = lax.broadcasted_iota(jnp.int32, (2 * TILE, TILE), 0) - lax.broadcasted_iota(
        jnp.int32, (2 * TILE, TILE), 1
    )
    band = jnp.where((gap >= AFTER - HW) & (gap <= AFTER + HW), 1.0, 0.0).astype(BF16)
    stride = channels // SRC_DEV
    row = lax.broadcasted_iota(jnp.int32, (16, channels), 0)
    col = lax.broadcasted_iota(jnp.int32, (16, channels), 1)
    pick = jnp.where((col == row * stride) & (row < SRC_DEV), 1.0, 0.0).astype(BF16)
    for t in range(0, FR, TILE):
        total = dot(hi[:, t : t + 2 * TILE], band) + dot(lo[:, t : t + 2 * TILE], band)
        level = total / (2 * HW + 1)
        center = filt_ref[:, AFTER + t : AFTER + t + TILE]
        white = (center / (level + EPS)).astype(BF16)
        for u in range(0, TILE, 128):
            q = (t + u) // 128
            part = white[:, u : u + 128]
            white_ref[channels * q : channels * (q + 1), :] = part
            back = dot(dot(pick, part).astype(BF16), flip).astype(BF16)
            for k in range(SRC_DEV):
                at = k * (FR // 128) + FR // 128 - 1 - q
                src_ref[at : at + 1, :] = back[k : k + 1]


def correlate_kernel(half_ref, white_ref, src_ref, *refs, scale, count, prior, narrow):
    refs = list(refs)
    sources, frames, _ = src_ref.shape
    group = sources // 2
    prior_ref = refs.pop(0) if prior else None
    out_refs = [refs.pop(0) for _ in range(count // group)]
    lhs_ref, nyq_ref, toep0_ref, toep1_ref, acc_ref = refs[:5]
    channels = nyq_ref.shape[1]
    sum_refs = refs[5:] if narrow else out_refs
    base = half_ref[0] * group
    blocks = FR // TILE
    toeps = (toep0_ref, toep1_ref)
    pad = jnp.zeros((1, TILE), F32)

    def place(s):
        return lax.rem(base + s, sources)

    def build(s, b):
        to_ref = toeps[s % 2]
        row = src_ref[place(s), b : b + 1, :]

        def store(h, rows):
            at = TILE * b + 16 * h
            to_ref[at : at + 16, :] = rows[:, TILE:]
            to_ref[at + 128 : at + 144, :] = rows[:, TILE - 128 : -128]

        strip(jnp.concatenate([pad, row, pad], 1), 1, store)

    odd = lax.broadcasted_iota(jnp.int32, (channels, 128), 1) % 2 == 1
    for b in range(frames):
        build(0, b)
        total = jnp.zeros((channels, 128), F32)
        for q in range(FR // 128):
            part = white_ref[b, channels * q : channels * (q + 1), :]
            to = channels * (q // 2)
            at = TILE * b + 128 * (q % 2)
            lhs_ref[to : to + channels, at : at + 128] = part
            total += part.astype(F32)
        nyq_ref[b] = jnp.sum(jnp.where(odd, -total, total), axis=1, keepdims=True)

    for s in range(count):
        toep_ref = toeps[s % 2]
        todo = list(range(frames)) if s + 1 < count else []
        for d in (0, 1, -1, 2, -2):
            at = TILE * (2 - d)
            first = channels * max(d, 0)
            rows = channels * (blocks - abs(d))
            res = dot(lhs_ref[first : first + rows, :], toep_ref[:, at : at + TILE])
            to = channels * max(-d, 0)
            if d == 0:
                acc_ref[...] = res
            else:
                acc_ref[to : to + rows, :] += res
            for b in todo[:1]:
                build(s + 1, b)
            todo = todo[1:]

        own = src_ref[place(s)]
        lane = lax.broadcasted_iota(jnp.int32, (frames, FR), 1)
        own_nyq = jnp.sum(jnp.where(lane % 2 == 1, own, -own), axis=1, keepdims=True)
        nyq = own_nyq[0:1] * nyq_ref[0]
        for b in range(1, frames):
            nyq += own_nyq[b : b + 1] * nyq_ref[b]
        nyq = jnp.broadcast_to(nyq, (channels, 128))
        nyq = jnp.where(odd, -nyq, nyq) * (scale / (2 * FR))
        for q in range(LAGS // 128):
            j, u = divmod(q, TILE // 128)
            lanes = slice(128 * u, 128 * (u + 1))
            part = acc_ref[channels * j : channels * (j + 1), lanes] * scale - nyq
            at = channels * (blocks * (s % group) + j)
            plain = slice(at, at + channels)
            if prior:
                rows = pl.ds(group * q + s, channels, stride=group * (LAGS // 128))
                sum_refs[0][rows, :] = part + prior_ref[plain, lanes]
            else:
                sum_refs[s // group][plain, lanes] = part
    if narrow:
        out_refs[0][...] = sum_refs[0][...].astype(BF16)


def correlate(half, bundle, src, channels, scale, count, prior=None, narrow=False):
    frames = bundle.shape[0]
    group = src.shape[0] // 2
    block = TILE if prior is None else 128
    shape = (channels * (LAGS // block) * group, block)
    whole = pl.BlockSpec(memory_space=pltpu.VMEM)
    extra = [] if prior is None else [prior]
    scratch = [
        pltpu.VMEM((FR // TILE * channels, TILE * frames), BF16),
        pltpu.VMEM((frames, channels, 1), F32),
        pltpu.VMEM((TILE * frames, 5 * TILE), BF16),
        pltpu.VMEM((TILE * frames, 5 * TILE), BF16),
        pltpu.VMEM((FR // TILE * channels, TILE), F32),
    ]
    if narrow:
        scratch.append(pltpu.VMEM(shape, F32))
    outs = count // group
    return pl.pallas_call(
        functools.partial(
            correlate_kernel, scale=scale, count=count, prior=prior is not None, narrow=narrow
        ),
        out_shape=[jax.ShapeDtypeStruct(shape, BF16 if narrow else F32)] * outs,
        in_specs=[pl.BlockSpec(memory_space=pltpu.SMEM)] + [whole] * (2 + len(extra)),
        out_specs=[whole] * outs,
        scratch_shapes=scratch,
        compiler_params=pltpu.CompilerParams(vmem_limit_bytes=28 << 20),
    )(half, bundle, src, *extra)


def on_device(raw, taps):
    samples, channels = raw.shape
    time_parts = lax.axis_size("tm")
    chan_parts = lax.axis_size("chan")
    chips = time_parts // 2
    place = lax.axis_index("tm")
    core = place % 2
    sources = SRC_DEV * chan_parts // chips
    scale = 1.0 / math.sqrt(samples * time_parts)
    up = [(i, i + 1) for i in range(time_parts - 1)]
    down = [(i + 1, i) for i in range(time_parts - 1)]
    before = lax.ppermute(raw, "tm", up)
    after = lax.ppermute(raw[:AFTER], "tm", down)
    last = (place == time_parts - 1).astype(jnp.int32).reshape(1)
    frame_rows = FR // 128
    whole = pl.BlockSpec(memory_space=pltpu.VMEM)
    white, src = pl.pallas_call(
        whiten_kernel,
        out_shape=(
            jax.ShapeDtypeStruct((frame_rows * channels, 128), BF16),
            jax.ShapeDtypeStruct((SRC_DEV * frame_rows, 128), BF16),
        ),
        grid=(1,),
        in_specs=[
            pl.BlockSpec(memory_space=pltpu.SMEM),
            whole,
            pl.BlockSpec((samples, channels), lambda i: (0, 0)),
            whole,
            pl.BlockSpec((1, TAPS), lambda i: (0, 0)),
        ],
        out_specs=(whole, whole),
        scratch_shapes=[
            pltpu.VMEM((TAPS + TILE, TILE), BF16),
            pltpu.VMEM((channels, BEFORE + FR + AFTER), BF16),
            pltpu.VMEM((channels, FR + 2 * AFTER), F32),
        ],
        compiler_params=pltpu.CompilerParams(vmem_limit_bytes=50 << 20),
    )(last, before, raw, after, taps[None])
    every = lax.all_to_all(
        jnp.broadcast_to(src[None], (chan_parts,) + src.shape), "chan", 0, 0, tiled=True
    )
    lines = chips // 2
    place = lax.optimization_barrier((place, every[0, 0, 0]))[0]
    core = place % 2
    side = place // 2 % 2
    every = every.reshape(lines, 2, sources * frame_rows, 128)
    mine = lax.dynamic_index_in_dim(every, side, 1, keepdims=False)
    others = lax.dynamic_index_in_dim(every, 1 - side, 1, keepdims=False)
    far = jnp.concatenate([white, others.reshape(-1, 128)], 0)
    far = lax.ppermute(far, "tm", [(i, i ^ 2) for i in range(time_parts)])
    groups = [[c + 4 * i for i in range(lines)] for c in range(4)]

    def gather(frame, srcs):
        both = jnp.concatenate([jnp.broadcast_to(frame[None], (lines,) + frame.shape), srcs], 1)
        return lax.all_to_all(both, "tm", 0, 0, tiled=True, axis_index_groups=groups)

    def signals(bundle):
        srcs = bundle[:, frame_rows * channels :].astype(F32)
        return srcs.reshape(lines, sources, FR).transpose(1, 0, 2)

    near = gather(white, mine)
    far = lax.optimization_barrier((far, near[0, 0, 0]))[0]
    far = gather(far[: white.shape[0]], far[white.shape[0] :].reshape(mine.shape))
    other = (1 - core).reshape(1)
    own = core.reshape(1)
    parts = correlate(other, near, signals(near), channels, scale, sources)
    half = sources // 2
    srcs = signals(far)
    theirs = correlate(other, far, srcs, channels, scale, half, parts[0], True)[0]
    theirs = lax.ppermute(theirs, "tm", [(i, i ^ 1) for i in range(time_parts)])
    ours = correlate(own, far, srcs, channels, scale, half, parts[1])[0]
    out = ours + theirs.astype(F32)
    out = out.reshape(channels, LAGS // 128, half, 128).transpose(0, 2, 1, 3)
    return out.reshape(channels, half, LAGS)


def solution(mesh):
    placed = (P("tm", "chan"), P())
    return jax.shard_map(
        on_device, mesh=mesh, in_specs=placed, out_specs=P("chan", "tm", None), check_vma=False
    )
```

```python
import functools
import math

import jax
import jax.numpy as jnp
from jax import lax
from jax.experimental import pallas as pl
from jax.experimental.pallas import tpu as pltpu
from jax.sharding import PartitionSpec as P

TAPS = 512
HW = 64
FR = 1024
LAGS = 1024
SRC_DEV = 2
BEFORE = 640
AFTER = 128
TILE = 256
EPS = 1e-05
BF16 = jnp.bfloat16
F32 = jnp.float32


def dot(a, b):
    return jnp.dot(a, b, preferred_element_type=F32)


def strip(row, first, store):
    width = row.shape[1]
    base = pltpu.roll(jnp.broadcast_to(row, (8, width)), first, 1, stride=1, stride_axis=0)
    for h in range(8):
        low = pltpu.roll(base, 16 * h, 1) if h else base
        high = pltpu.roll(base, 16 * h + 8, 1)
        store(h, jnp.concatenate([low, high], 0).astype(BF16))


def whiten_kernel(
    last_ref, before_ref, raw_ref, after_ref, taps_ref, white_ref, src_ref, toep_ref, rawt_ref, filt_ref
):
    channels = raw_ref.shape[1]
    toep_rows = TAPS + TILE
    r = lax.broadcasted_iota(jnp.int32, (128, 128), 0)
    c = lax.broadcasted_iota(jnp.int32, (128, 128), 1)
    flip = jnp.where(r + c == 127, 1.0, 0.0).astype(BF16)
    taps = jnp.broadcast_to(taps_ref[...].astype(F32), (16, TAPS)).astype(BF16)
    parts = [jnp.zeros((1, 128), F32)]
    parts += [dot(taps[:, t - 128 : t], flip)[:1] for t in range(TAPS, 0, -128)]
    parts += [jnp.zeros((1, 384), F32)]

    def store(h, rows):
        for a in range(toep_rows // 128):
            at = BEFORE - 128 * a
            toep_ref[128 * a + 16 * h : 128 * a + 16 * h + 16, :] = rows[:, at : at + TILE]

    strip(jnp.concatenate(parts, 1), 0, store)
    rawt_ref[:, :BEFORE] = before_ref[FR - BEFORE :, :].T
    rawt_ref[:, BEFORE : BEFORE + FR] = raw_ref[...].T
    rawt_ref[:, BEFORE + FR :] = after_ref[...].T
    toep = toep_ref[...]
    span = FR + 2 * AFTER
    for y in range(0, span, TILE):
        filt_ref[:, y : y + TILE] = dot(rawt_ref[:, y : y + toep_rows], toep)
    past = lax.broadcasted_iota(jnp.int32, (channels, AFTER), 0) * 0 + last_ref[0]
    filt_ref[:, span - AFTER :] = jnp.where(past == 1, 0.0, filt_ref[:, span - AFTER :])
    size = jnp.abs(filt_ref[...])
    hi = size.astype(BF16)
    lo = (size - hi.astype(F32)).astype(BF16)
    gap = lax.broadcasted_iota(jnp.int32, (2 * TILE, TILE), 0) - lax.broadcasted_iota(
        jnp.int32, (2 * TILE, TILE), 1
    )
    band = jnp.where((gap >= AFTER - HW) & (gap <= AFTER + HW), 1.0, 0.0).astype(BF16)
    stride = channels // SRC_DEV
    row = lax.broadcasted_iota(jnp.int32, (16, channels), 0)
    col = lax.broadcasted_iota(jnp.int32, (16, channels), 1)
    pick = jnp.where((col == row * stride) & (row < SRC_DEV), 1.0, 0.0).astype(BF16)
    for t in range(0, FR, TILE):
        total = dot(hi[:, t : t + 2 * TILE], band) + dot(lo[:, t : t + 2 * TILE], band)
        level = total / (2 * HW + 1)
        center = filt_ref[:, AFTER + t : AFTER + t + TILE]
        white = (center / (level + EPS)).astype(BF16)
        for u in range(0, TILE, 128):
            q = (t + u) // 128
            part = white[:, u : u + 128]
            white_ref[channels * q : channels * (q + 1), :] = part
            back = dot(dot(pick, part).astype(BF16), flip).astype(BF16)
            for k in range(SRC_DEV):
                at = k * (FR // 128) + FR // 128 - 1 - q
                src_ref[at : at + 1, :] = back[k : k + 1]


def correlate_kernel(half_ref, white_ref, src_ref, *refs, scale, count, prior, narrow):
    refs = list(refs)
    frames, src_rows, _ = src_ref.shape
    frame_rows = FR // 128
    sources = src_rows // frame_rows
    group = sources // 2
    prior_ref = refs.pop(0) if prior else None
    out_refs = [refs.pop(0) for _ in range(count // group)]
    lhs_ref, nyq_ref, toep0_ref, toep1_ref, acc_ref = refs[:5]
    channels = nyq_ref.shape[1]
    sum_refs = refs[5:] if narrow else out_refs
    base = half_ref[0] * group
    blocks = FR // TILE
    toeps = (toep0_ref, toep1_ref)
    pad = jnp.zeros((1, TILE), F32)

    def signal(s, b):
        at = pl.multiple_of(lax.rem(base + s, sources) * frame_rows, frame_rows)
        return src_ref[b, pl.ds(at, frame_rows), :]

    def build(s, b):
        to_ref = toeps[s % 2]
        rows = signal(s, b)
        row = jnp.concatenate([rows[q : q + 1] for q in range(frame_rows)], 1)

        def store(h, rows):
            at = TILE * b + 16 * h
            to_ref[at : at + 16, :] = rows[:, TILE:]
            to_ref[at + 128 : at + 144, :] = rows[:, TILE - 128 : -128]

        strip(jnp.concatenate([pad, row, pad], 1), 1, store)

    odd = lax.broadcasted_iota(jnp.int32, (channels, 128), 1) % 2 == 1
    for b in range(frames):
        build(0, b)
        total = jnp.zeros((channels, 128), F32)
        for q in range(FR // 128):
            part = white_ref[b, channels * q : channels * (q + 1), :]
            to = channels * (q // 2)
            at = TILE * b + 128 * (q % 2)
            lhs_ref[to : to + channels, at : at + 128] = part
            total += part.astype(F32)
        nyq_ref[b] = jnp.sum(jnp.where(odd, -total, total), axis=1, keepdims=True)

    for s in range(count):
        toep_ref = toeps[s % 2]
        todo = list(range(frames)) if s + 1 < count else []
        for d in (0, 1, -1, 2, -2):
            at = TILE * (2 - d)
            first = channels * max(d, 0)
            rows = channels * (blocks - abs(d))
            res = dot(lhs_ref[first : first + rows, :], toep_ref[:, at : at + TILE])
            to = channels * max(-d, 0)
            if d == 0:
                acc_ref[...] = res
            else:
                acc_ref[to : to + rows, :] += res
            for b in todo[:1]:
                build(s + 1, b)
            todo = todo[1:]

        nyq = jnp.zeros((channels, 1), F32)
        for b in range(frames):
            own = signal(s, b)
            own = jnp.sum(jnp.where(odd[:frame_rows], own, -own), axis=1, keepdims=True)
            nyq += jnp.sum(own, axis=0, keepdims=True) * nyq_ref[b]
        nyq = jnp.broadcast_to(nyq, (channels, 128))
        nyq = jnp.where(odd, -nyq, nyq) * (scale / (2 * FR))
        for q in range(LAGS // 128):
            j, u = divmod(q, TILE // 128)
            lanes = slice(128 * u, 128 * (u + 1))
            part = acc_ref[channels * j : channels * (j + 1), lanes] * scale - nyq
            at = channels * (blocks * (s % group) + j)
            plain = slice(at, at + channels)
            if prior:
                rows = pl.ds(group * q + s, channels, stride=group * (LAGS // 128))
                sum_refs[0][rows, :] = part + prior_ref[plain, lanes].astype(F32)
            else:
                sum_refs[s // group][plain, lanes] = part.astype(sum_refs[0].dtype)
    if narrow:
        out_refs[0][...] = sum_refs[0][...].astype(BF16)


def correlate(half, bundle, src, channels, scale, count, prior=None, narrow=False):
    frames = bundle.shape[0]
    group = src.shape[1] // (FR // 128) // 2
    block = TILE if prior is None else 128
    shape = (channels * (LAGS // block) * group, block)
    whole = pl.BlockSpec(memory_space=pltpu.VMEM)
    extra = [] if prior is None else [prior]
    scratch = [
        pltpu.VMEM((FR // TILE * channels, TILE * frames), BF16),
        pltpu.VMEM((frames, channels, 1), F32),
        pltpu.VMEM((TILE * frames, 5 * TILE), BF16),
        pltpu.VMEM((TILE * frames, 5 * TILE), BF16),
        pltpu.VMEM((FR // TILE * channels, TILE), F32),
    ]
    if narrow:
        scratch.append(pltpu.VMEM(shape, F32))
    outs = count // group
    return pl.pallas_call(
        functools.partial(
            correlate_kernel, scale=scale, count=count, prior=prior is not None, narrow=narrow
        ),
        out_shape=[jax.ShapeDtypeStruct(shape, BF16 if narrow or prior is None else F32)] * outs,
        in_specs=[pl.BlockSpec(memory_space=pltpu.SMEM)] + [whole] * (2 + len(extra)),
        out_specs=[whole] * outs,
        scratch_shapes=scratch,
        compiler_params=pltpu.CompilerParams(vmem_limit_bytes=28 << 20),
    )(half, bundle, src, *extra)


def on_device(raw, taps):
    samples, channels = raw.shape
    time_parts = lax.axis_size("tm")
    chan_parts = lax.axis_size("chan")
    chips = time_parts // 2
    place = lax.axis_index("tm")
    core = place % 2
    sources = SRC_DEV * chan_parts // chips
    scale = 1.0 / math.sqrt(samples * time_parts)
    up = [(i, i + 1) for i in range(time_parts - 1)]
    down = [(i + 1, i) for i in range(time_parts - 1)]
    before = lax.ppermute(raw, "tm", up)
    after = lax.ppermute(raw[:AFTER], "tm", down)
    last = (place == time_parts - 1).astype(jnp.int32).reshape(1)
    frame_rows = FR // 128
    whole = pl.BlockSpec(memory_space=pltpu.VMEM)
    white, src = pl.pallas_call(
        whiten_kernel,
        out_shape=(
            jax.ShapeDtypeStruct((frame_rows * channels, 128), BF16),
            jax.ShapeDtypeStruct((SRC_DEV * frame_rows, 128), BF16),
        ),
        grid=(1,),
        in_specs=[
            pl.BlockSpec(memory_space=pltpu.SMEM),
            whole,
            pl.BlockSpec((samples, channels), lambda i: (0, 0)),
            whole,
            pl.BlockSpec((1, TAPS), lambda i: (0, 0)),
        ],
        out_specs=(whole, whole),
        scratch_shapes=[
            pltpu.VMEM((TAPS + TILE, TILE), BF16),
            pltpu.VMEM((channels, BEFORE + FR + AFTER), BF16),
            pltpu.VMEM((channels, FR + 2 * AFTER), F32),
        ],
        compiler_params=pltpu.CompilerParams(vmem_limit_bytes=50 << 20),
    )(last, before, raw, after, taps[None])
    every = lax.all_to_all(
        jnp.broadcast_to(src[None], (chan_parts,) + src.shape), "chan", 0, 0, tiled=True
    )
    lines = chips // 2
    place, white, _ = lax.optimization_barrier((place, white, every[0, 0, 0]))
    core = place % 2
    side = place // 2 % 2
    every = every.reshape(lines, 2, sources * frame_rows, 128)
    mine = lax.dynamic_index_in_dim(every, side, 1, keepdims=False)
    others = lax.dynamic_index_in_dim(every, 1 - side, 1, keepdims=False)
    far = jnp.concatenate([white, others.reshape(-1, 128)], 0)
    far = lax.ppermute(far, "tm", [(i, i ^ 2) for i in range(time_parts)])
    groups = [[c + 4 * i for i in range(lines)] for c in range(4)]

    def gather(frame, srcs):
        both = jnp.concatenate([jnp.broadcast_to(frame[None], (lines,) + frame.shape), srcs], 1)
        return lax.all_to_all(both, "tm", 0, 0, tiled=True, axis_index_groups=groups)

    def signals(bundle):
        return bundle[:, frame_rows * channels :].astype(F32)

    near = gather(white, mine)
    far = lax.optimization_barrier((far, near[0, 0, 0]))[0]
    far = gather(far[: white.shape[0]], far[white.shape[0] :].reshape(mine.shape))
    other = (1 - core).reshape(1)
    own = core.reshape(1)
    parts = correlate(other, near, signals(near), channels, scale, sources)
    half = sources // 2
    srcs = signals(far)
    theirs = correlate(other, far, srcs, channels, scale, half, parts[0], True)[0]
    theirs = lax.ppermute(theirs, "tm", [(i, i ^ 1) for i in range(time_parts)])
    ours = correlate(own, far, srcs, channels, scale, half, parts[1])[0]
    out = ours + theirs.astype(F32)
    out = out.reshape(channels, LAGS // 128, half, 128).transpose(0, 2, 1, 3)
    return out.reshape(channels, half, LAGS)


def solution(mesh):
    placed = (P("tm", "chan"), P())
    return jax.shard_map(
        on_device, mesh=mesh, in_specs=placed, out_specs=P("chan", "tm", None), check_vma=False
    )
```

```python
import functools
import math

import jax
import jax.numpy as jnp
from jax import lax
from jax.experimental import pallas as pl
from jax.experimental.pallas import tpu as pltpu
from jax.sharding import PartitionSpec as P

TAPS = 512
HW = 64
FR = 1024
LAGS = 1024
SRC_DEV = 2
BEFORE = 640
AFTER = 128
TILE = 256
EPS = 1e-05
BF16 = jnp.bfloat16
F32 = jnp.float32


def dot(a, b):
    return jnp.dot(a, b, preferred_element_type=F32)


def strip(row, first, store):
    width = row.shape[1]
    base = pltpu.roll(jnp.broadcast_to(row, (8, width)), first, 1, stride=1, stride_axis=0)
    for h in range(8):
        low = pltpu.roll(base, 16 * h, 1) if h else base
        high = pltpu.roll(base, 16 * h + 8, 1)
        store(h, jnp.concatenate([low, high], 0).astype(BF16))


def whiten_kernel(
    last_ref, before_ref, raw_ref, after_ref, taps_ref, white_ref, src_ref, toep_ref, rawt_ref, filt_ref
):
    channels = raw_ref.shape[1]
    toep_rows = TAPS + TILE
    r = lax.broadcasted_iota(jnp.int32, (128, 128), 0)
    c = lax.broadcasted_iota(jnp.int32, (128, 128), 1)
    flip = jnp.where(r + c == 127, 1.0, 0.0).astype(BF16)
    taps = jnp.broadcast_to(taps_ref[...].astype(F32), (16, TAPS)).astype(BF16)
    parts = [jnp.zeros((1, 128), F32)]
    parts += [dot(taps[:, t - 128 : t], flip)[:1] for t in range(TAPS, 0, -128)]
    parts += [jnp.zeros((1, 384), F32)]

    def store(h, rows):
        for a in range(toep_rows // 128):
            at = BEFORE - 128 * a
            toep_ref[128 * a + 16 * h : 128 * a + 16 * h + 16, :] = rows[:, at : at + TILE]

    strip(jnp.concatenate(parts, 1), 0, store)
    rawt_ref[:, :BEFORE] = before_ref[FR - BEFORE :, :].T
    rawt_ref[:, BEFORE : BEFORE + FR] = raw_ref[...].T
    rawt_ref[:, BEFORE + FR :] = after_ref[...].T
    toep = toep_ref[...]
    span = FR + 2 * AFTER
    for y in range(0, span, TILE):
        filt_ref[:, y : y + TILE] = dot(rawt_ref[:, y : y + toep_rows], toep)
    past = lax.broadcasted_iota(jnp.int32, (channels, AFTER), 0) * 0 + last_ref[0]
    filt_ref[:, span - AFTER :] = jnp.where(past == 1, 0.0, filt_ref[:, span - AFTER :])
    size = jnp.abs(filt_ref[...])
    hi = size.astype(BF16)
    lo = (size - hi.astype(F32)).astype(BF16)
    gap = lax.broadcasted_iota(jnp.int32, (2 * TILE, TILE), 0) - lax.broadcasted_iota(
        jnp.int32, (2 * TILE, TILE), 1
    )
    band = jnp.where((gap >= AFTER - HW) & (gap <= AFTER + HW), 1.0, 0.0).astype(BF16)
    stride = channels // SRC_DEV
    row = lax.broadcasted_iota(jnp.int32, (16, channels), 0)
    col = lax.broadcasted_iota(jnp.int32, (16, channels), 1)
    pick = jnp.where((col == row * stride) & (row < SRC_DEV), 1.0, 0.0).astype(BF16)
    for t in range(0, FR, TILE):
        total = dot(hi[:, t : t + 2 * TILE], band) + dot(lo[:, t : t + 2 * TILE], band)
        level = total / (2 * HW + 1)
        center = filt_ref[:, AFTER + t : AFTER + t + TILE]
        white = (center / (level + EPS)).astype(BF16)
        for u in range(0, TILE, 128):
            q = (t + u) // 128
            part = white[:, u : u + 128]
            white_ref[channels * q : channels * (q + 1), :] = part
            back = dot(dot(pick, part).astype(BF16), flip).astype(BF16)
            for k in range(SRC_DEV):
                at = k * (FR // 128) + FR // 128 - 1 - q
                src_ref[at : at + 1, :] = back[k : k + 1]


def correlate_kernel(half_ref, white_ref, src_ref, *refs, scale, count, prior, narrow):
    refs = list(refs)
    frames, src_rows, _ = src_ref.shape
    frame_rows = FR // 128
    sources = src_rows // frame_rows
    group = sources // 2
    prior_ref = refs.pop(0) if prior else None
    out_refs = [refs.pop(0) for _ in range(count // group)]
    lhs_ref, nyq_ref, toep0_ref, toep1_ref, acc_ref = refs[:5]
    channels = nyq_ref.shape[1]
    sum_refs = refs[5:] if narrow else out_refs
    base = half_ref[0] * group
    blocks = FR // TILE
    toeps = (toep0_ref, toep1_ref)
    pad = jnp.zeros((1, TILE), F32)

    def signal(s, b):
        at = pl.multiple_of(lax.rem(base + s, sources) * frame_rows, frame_rows)
        return src_ref[b, pl.ds(at, frame_rows), :]

    def build(s, b):
        to_ref = toeps[s % 2]
        rows = signal(s, b)
        row = jnp.concatenate([rows[q : q + 1] for q in range(frame_rows)], 1)

        def store(h, rows):
            at = TILE * b + 16 * h
            to_ref[at : at + 16, :] = rows[:, TILE:]
            to_ref[at + 128 : at + 144, :] = rows[:, TILE - 128 : -128]

        strip(jnp.concatenate([pad, row, pad], 1), 1, store)

    odd = lax.broadcasted_iota(jnp.int32, (channels, 128), 1) % 2 == 1
    for b in range(frames):
        build(0, b)
        total = jnp.zeros((channels, 128), F32)
        for q in range(FR // 128):
            part = white_ref[b, channels * q : channels * (q + 1), :]
            to = channels * (q // 2)
            at = TILE * b + 128 * (q % 2)
            lhs_ref[to : to + channels, at : at + 128] = part
            total += part.astype(F32)
        nyq_ref[b] = jnp.sum(jnp.where(odd, -total, total), axis=1, keepdims=True)

    for s in range(count):
        toep_ref = toeps[s % 2]
        todo = list(range(frames)) if s + 1 < count else []
        for d in (0, 1, -1, 2, -2):
            at = TILE * (2 - d)
            first = channels * max(d, 0)
            rows = channels * (blocks - abs(d))
            res = dot(lhs_ref[first : first + rows, :], toep_ref[:, at : at + TILE])
            to = channels * max(-d, 0)
            if d == 0:
                acc_ref[...] = res
            else:
                acc_ref[to : to + rows, :] += res
            for b in todo[:1]:
                build(s + 1, b)
            todo = todo[1:]

        nyq = jnp.zeros((channels, 1), F32)
        for b in range(frames):
            own = signal(s, b)
            own = jnp.sum(jnp.where(odd[:frame_rows], own, -own), axis=1, keepdims=True)
            nyq += jnp.sum(own, axis=0, keepdims=True) * nyq_ref[b]
        nyq = jnp.broadcast_to(nyq, (channels, 128))
        nyq = jnp.where(odd, -nyq, nyq) * (scale / (2 * FR))
        for q in range(LAGS // 128):
            j, u = divmod(q, TILE // 128)
            lanes = slice(128 * u, 128 * (u + 1))
            part = acc_ref[channels * j : channels * (j + 1), lanes] * scale - nyq
            at = channels * (blocks * (s % group) + j)
            plain = slice(at, at + channels)
            if prior:
                rows = pl.ds(group * q + s, channels, stride=group * (LAGS // 128))
                sum_refs[0][rows, :] = part + prior_ref[plain, lanes].astype(F32)
            else:
                sum_refs[s // group][plain, lanes] = part.astype(sum_refs[0].dtype)
    if narrow:
        out_refs[0][...] = sum_refs[0][...].astype(BF16)


def correlate(half, bundle, src, channels, scale, count, prior=None, narrow=False):
    frames = bundle.shape[0]
    group = src.shape[1] // (FR // 128) // 2
    block = TILE if prior is None else 128
    shape = (channels * (LAGS // block) * group, block)
    whole = pl.BlockSpec(memory_space=pltpu.VMEM)
    extra = [] if prior is None else [prior]
    scratch = [
        pltpu.VMEM((FR // TILE * channels, TILE * frames), BF16),
        pltpu.VMEM((frames, channels, 1), F32),
        pltpu.VMEM((TILE * frames, 5 * TILE), BF16),
        pltpu.VMEM((TILE * frames, 5 * TILE), BF16),
        pltpu.VMEM((FR // TILE * channels, TILE), F32),
    ]
    if narrow:
        scratch.append(pltpu.VMEM(shape, F32))
    outs = count // group
    return pl.pallas_call(
        functools.partial(
            correlate_kernel, scale=scale, count=count, prior=prior is not None, narrow=narrow
        ),
        out_shape=[jax.ShapeDtypeStruct(shape, BF16 if narrow or prior is None else F32)] * outs,
        in_specs=[pl.BlockSpec(memory_space=pltpu.SMEM)] + [whole] * (2 + len(extra)),
        out_specs=[whole] * outs,
        scratch_shapes=scratch,
        compiler_params=pltpu.CompilerParams(vmem_limit_bytes=28 << 20),
    )(half, bundle, src, *extra)


def on_device(raw, taps):
    samples, channels = raw.shape
    time_parts = lax.axis_size("tm")
    chan_parts = lax.axis_size("chan")
    chips = time_parts // 2
    place = lax.axis_index("tm")
    core = place % 2
    sources = SRC_DEV * chan_parts // chips
    scale = 1.0 / math.sqrt(samples * time_parts)
    up = [(i, i + 1) for i in range(time_parts - 1)]
    down = [(i + 1, i) for i in range(time_parts - 1)]
    before = lax.ppermute(raw, "tm", up)
    after = lax.ppermute(raw[:AFTER], "tm", down)
    last = (place == time_parts - 1).astype(jnp.int32).reshape(1)
    frame_rows = FR // 128
    whole = pl.BlockSpec(memory_space=pltpu.VMEM)
    white, src = pl.pallas_call(
        whiten_kernel,
        out_shape=(
            jax.ShapeDtypeStruct((frame_rows * channels, 128), BF16),
            jax.ShapeDtypeStruct((SRC_DEV * frame_rows, 128), BF16),
        ),
        grid=(1,),
        in_specs=[
            pl.BlockSpec(memory_space=pltpu.SMEM),
            whole,
            pl.BlockSpec((samples, channels), lambda i: (0, 0)),
            whole,
            pl.BlockSpec((1, TAPS), lambda i: (0, 0)),
        ],
        out_specs=(whole, whole),
        scratch_shapes=[
            pltpu.VMEM((TAPS + TILE, TILE), BF16),
            pltpu.VMEM((channels, BEFORE + FR + AFTER), BF16),
            pltpu.VMEM((channels, FR + 2 * AFTER), F32),
        ],
        compiler_params=pltpu.CompilerParams(vmem_limit_bytes=50 << 20),
    )(last, before, raw, after, taps[None])
    lines = chips // 2
    near_side = (place // 2 % 2).astype(F32)
    own = core.reshape(1)
    other = (1 - core).reshape(1)
    src, near_side, own, other = lax.optimization_barrier((src, near_side, own, other))
    every = lax.all_to_all(
        jnp.broadcast_to(src[None], (chan_parts,) + src.shape), "chan", 0, 0, tiled=True
    )
    every = every.reshape(lines, 2, sources * frame_rows, 128)
    white, every = lax.optimization_barrier((white, every))
    second = near_side > 0.5
    mine = jnp.where(second, every[:, 1], every[:, 0])
    others = jnp.where(second, every[:, 0], every[:, 1])
    far = jnp.concatenate([white, others.reshape(-1, 128)], 0)
    groups = [[c + 4 * i for i in range(lines)] for c in range(4)]

    def bundled(frame, srcs):
        return jnp.concatenate([jnp.broadcast_to(frame[None], (lines,) + frame.shape), srcs], 1)

    def gather(bundle):
        return lax.all_to_all(bundle, "tm", 0, 0, tiled=True, axis_index_groups=groups)

    def signals(bundle):
        return bundle[:, frame_rows * channels :].astype(F32)

    near, far = lax.optimization_barrier((bundled(white, mine), far))
    far = lax.ppermute(far, "tm", [(i, i ^ 2) for i in range(time_parts)])
    near = gather(near)
    far = bundled(far[: white.shape[0]], far[white.shape[0] :].reshape(mine.shape))
    far = gather(lax.optimization_barrier((far, near[0, 0, 0]))[0])
    parts = correlate(other, near, signals(near), channels, scale, sources)
    half = sources // 2
    srcs = signals(far)
    theirs = correlate(other, far, srcs, channels, scale, half, parts[0], True)[0]
    theirs = lax.ppermute(theirs, "tm", [(i, i ^ 1) for i in range(time_parts)])
    ours = correlate(own, far, srcs, channels, scale, half, parts[1])[0]
    out = ours + theirs.astype(F32)
    out = out.reshape(channels, LAGS // 128, half, 128).transpose(0, 2, 1, 3)
    return out.reshape(channels, half, LAGS)


def solution(mesh):
    placed = (P("tm", "chan"), P())
    return jax.shard_map(
        on_device, mesh=mesh, in_specs=placed, out_specs=P("chan", "tm", None), check_vma=False
    )
```
